256 devices in a mesh: band: 4 (over x), dom: 64 (over z, y, core).
Axes of the slice: x: 4, y: 4, z: 8, core: 2. Of those that a mesh axis runs over, the one named last changes fastest.
Arguments:
- orbitals: bfloat16 [256, 512, 2048], P('dom', None, 'band'), may hold values from -6 to 6
- projector_blocks: bfloat16 [4, 64, 96, 256, 128], P('band', 'dom'), may hold values from -0.1875 to 0.1875
- block_rows: int32 [4, 64, 96], P('band', 'dom'), may hold values from 0 to 15, as said below
- block_cols: int32 [4, 64, 96], P('band', 'dom'), may hold values from 0 to 26
- block_counts: int32 [4, 64], P('band', 'dom'), may hold values from 16 to 96, as said below
- strengths: float32 [73728], P('dom'), may hold values from -1.5 to 1.5
Outputs:
- applied: bfloat16 [256, 512, 2048], P('dom', None, 'band')
The draws below stay inside these ranges and needn't reach their ends.
Inputs may be any that keep to these rules, and one draw needn't show every extreme that they name: `block_rows`: the slots of one device name distinct pairs of row block and column block. `block_counts`: some device has all 96 slots live.
All inputs are finite; a program needn't handle non-finite values.
Results may differ from the reference program's by a relative error of at most 0.0049.
Values may be sent and summed in bfloat16 or wider, within the bound.
A program may use at most 128 MiB of HBM per device.

```python
import jax
import jax.numpy as jnp
from jax import lax

STATES = 256
ZP = 8
CROSS = 512
RB = 256
CB = 128
CBS = 9
NBMAX = 96
ZN = 512
XR = 2048
PCOL = 1152
N_BAND = 4
N_DOM = 64


def block_pairs(key):
    total = ZP * CROSS // RB * 3 * CBS
    keys = jax.random.split(jax.random.fold_in(key, 7), N_BAND * N_DOM)
    chosen = jax.vmap(lambda single: jax.random.permutation(single, total)[:NBMAX])(keys)
    return chosen.reshape(N_BAND, N_DOM, NBMAX).astype(jnp.int32)


def draw_block_rows(key, part):
    return (block_pairs(key) // (3 * CBS)).astype(jnp.int32)


def draw_block_cols(key, part):
    return (block_pairs(key) % (3 * CBS)).astype(jnp.int32)


def draw_block_counts(key, part):
    lowest = NBMAX // 6
    spread = NBMAX - lowest
    raw = jax.random.randint(jax.random.fold_in(key, 11), (N_BAND, N_DOM), 0, spread + 1)
    loads = lowest + raw * raw * raw // (spread * spread)
    busiest = jax.random.randint(jax.random.fold_in(key, 13), (), 0, N_BAND * N_DOM)
    flat_index = jnp.arange(N_BAND * N_DOM, dtype=jnp.int32).reshape(N_BAND, N_DOM)
    return jnp.where(flat_index == busiest, NBMAX, loads).astype(jnp.int32)


def block_levels(own_key, dims, cuts, least, largest):
    level = 1.0
    for axis_at, shards_of in cuts:
        heights = jax.random.uniform(jax.random.fold_in(jax.random.fold_in(own_key, 6), axis_at), (shards_of,), jnp.float32, least / len(cuts), largest / len(cuts))
        level = level * jnp.repeat(jnp.exp(heights), dims[axis_at] // shards_of).reshape((-1,) + (1,) * (len(dims) - 1 - axis_at))
    return level


def centred(rng, extent, deviation, bound, pieces=(), held_as=jnp.bfloat16):
    factor_of = block_levels(rng, extent, pieces, -0.22, 0.18) if pieces else 1.0
    result = jax.random.normal(rng, extent, jnp.float32) * deviation * factor_of
    return jnp.minimum(jnp.maximum(result, -bound), bound).astype(held_as)


def setup_inputs(seed: int = 0) -> dict:
    splits = jax.random.split(jax.random.key(seed), 7)
    orbitals = centred(splits[0], (STATES, ZN, XR), 1.0, 6.0, ((0, 64), (2, 4)))
    projector_blocks = centred(splits[1], (N_BAND, N_DOM, NBMAX, RB, CB), 1024 ** -0.5, 0.1875, ((0, 4), (1, 64)))
    block_rows = draw_block_rows(jax.random.fold_in(splits[6], 71), 0)
    block_cols = draw_block_cols(jax.random.fold_in(splits[6], 71), 0)
    block_counts = draw_block_counts(jax.random.fold_in(splits[6], 71), 0)
    strengths = jnp.clip(jax.random.uniform(splits[5], (N_DOM * PCOL,), jnp.float32, -1.5, 1.5) * block_levels(splits[5], (N_DOM * PCOL,), ((0, 64),), -0.4, 0.0), -1.5, 1.5)
    return dict(orbitals=orbitals, projector_blocks=projector_blocks, block_rows=block_rows, block_cols=block_cols, block_counts=block_counts, strengths=strengths)


def reference(orbitals, projector_blocks, block_rows, block_cols, block_counts, strengths):
    row_blocks = ZP * CROSS // RB
    devices_all = N_BAND * N_DOM
    by_device = orbitals.reshape(STATES, N_DOM, ZP, N_BAND, CROSS).transpose(3, 1, 0, 2, 4)
    by_device = by_device.reshape(devices_all, STATES, row_blocks, RB)
    weights = projector_blocks.reshape(devices_all, NBMAX, RB, CB)
    slot_rows = block_rows.reshape(devices_all, NBMAX).astype(jnp.int32)
    slot_cols = block_cols.reshape(devices_all, NBMAX).astype(jnp.int32)
    live_counts = block_counts.reshape(devices_all).astype(jnp.int32)
    dom_index = jnp.tile(jnp.arange(N_DOM, dtype=jnp.int32), N_BAND)
    slab_of = (dom_index[:, None] + slot_cols // CBS - 1) % N_DOM
    targets = (slab_of * CBS + slot_cols % CBS).astype(jnp.int32)
    slots = jnp.arange(NBMAX, dtype=jnp.int32)

    def forward(carry, inputs):
        states_dev, weight_dev, rows_dev, count_dev, target_dev = inputs
        picked = jnp.take(states_dev, rows_dev, axis=1)
        term = jnp.einsum('skr,krc->kcs', picked.astype(jnp.float32), weight_dev.astype(jnp.float32))
        weight_live = (slots < count_dev).astype(jnp.float32)
        carry = carry.at[target_dev].add(term * weight_live[:, None, None])
        return carry, None

    start = jnp.zeros((N_DOM * CBS, CB, STATES), jnp.float32)
    coef, _ = lax.scan(forward, start, (by_device, weights, slot_rows, live_counts, targets))
    chi = (strengths.reshape(N_DOM * CBS, CB)[:, :, None] * coef).astype(jnp.bfloat16)

    def backward(carry, inputs):
        weight_dev, rows_dev, count_dev, target_dev = inputs
        chosen = chi[target_dev]
        term = jnp.einsum('krc,kcs->ksr', weight_dev.astype(jnp.float32), chosen.astype(jnp.float32))
        weight_live = (slots < count_dev).astype(jnp.float32)
        term = term * weight_live[:, None, None]
        placed = jnp.zeros((STATES, row_blocks, RB), jnp.float32).at[:, rows_dev, :].add(term.transpose(1, 0, 2))
        return carry, placed.astype(jnp.bfloat16)

    _, outputs = lax.scan(backward, jnp.zeros((), jnp.float32), (weights, slot_rows, live_counts, targets))
    outputs = outputs.reshape(N_BAND, N_DOM, STATES, ZP, CROSS).transpose(2, 1, 3, 0, 4)
    return outputs.reshape(STATES, ZP * N_DOM, CROSS * N_BAND)
```

```python
import jax
import jax.numpy as jnp
from jax import lax
from jax.experimental import pallas as pl
from jax.experimental.pallas import tpu as pltpu
from jax.sharding import PartitionSpec as P


def passed_along(value, axis, steps):
    count = lax.axis_size(axis)
    pairs = [(source, (source + steps) % count) for source in range(count)]
    return lax.ppermute(value, axis, pairs)


def project_kernel(rows_ref, cols_ref, count_ref, states_ref, weights_ref, out_ref):
    out_ref[...] = jnp.zeros_like(out_ref)

    def body(k, carry):
        row = rows_ref[k]
        col = cols_ref[k]
        out_ref[col] += jnp.dot(states_ref[row], weights_ref[k], preferred_element_type=jnp.float32)
        return carry

    lax.fori_loop(0, count_ref[0], body, 0)


def apply_kernel(rows_ref, cols_ref, count_ref, chi_ref, weights_ref, out_ref, acc_ref):
    acc_ref[...] = jnp.zeros_like(acc_ref)

    def body(k, carry):
        row = rows_ref[k]
        col = cols_ref[k]
        acc_ref[row] += lax.dot_general(
            chi_ref[col], weights_ref[k], (((1,), (1,)), ((), ())), preferred_element_type=jnp.float32
        )
        return carry

    lax.fori_loop(0, count_ref[0], body, 0)
    out_ref[...] = acc_ref[...].astype(out_ref.dtype)


def smem():
    return pl.BlockSpec(memory_space=pltpu.SMEM)


def vmem():
    return pl.BlockSpec(memory_space=pltpu.VMEM)


def project(rows, cols, count, states, weights, col_blocks):
    row_blocks, state_total, row_width = states.shape
    slot_total, _, col_width = weights.shape
    flops = 2 * slot_total * state_total * row_width * col_width
    moved = states.size * 2 + weights.size * 2 + col_blocks * state_total * col_width * 4
    return pl.pallas_call(
        project_kernel,
        out_shape=jax.ShapeDtypeStruct((col_blocks, state_total, col_width), jnp.float32),
        in_specs=[smem(), smem(), smem(), vmem(), vmem()],
        out_specs=vmem(),
        compiler_params=pltpu.CompilerParams(vmem_limit_bytes=60 * 1024 * 1024),
        cost_estimate=pl.CostEstimate(flops=flops, bytes_accessed=moved, transcendentals=0),
    )(rows, cols, count, states, weights)


def apply(rows, cols, count, chi, weights, row_blocks):
    col_blocks, state_total, col_width = chi.shape
    slot_total, row_width, _ = weights.shape
    flops = 2 * slot_total * state_total * row_width * col_width
    moved = chi.size * 2 + weights.size * 2 + row_blocks * state_total * row_width * 2
    return pl.pallas_call(
        apply_kernel,
        out_shape=jax.ShapeDtypeStruct((row_blocks, state_total, row_width), jnp.bfloat16),
        in_specs=[smem(), smem(), smem(), vmem(), vmem()],
        out_specs=vmem(),
        scratch_shapes=[pltpu.VMEM((row_blocks, state_total, row_width), jnp.float32)],
        compiler_params=pltpu.CompilerParams(vmem_limit_bytes=60 * 1024 * 1024),
        cost_estimate=pl.CostEstimate(flops=flops, bytes_accessed=moved, transcendentals=0),
    )(rows, cols, count, chi, weights)


def per_device(orbitals, projector_blocks, block_rows, block_cols, block_counts, strengths):
    dom = lax.axis_size("dom")
    local_states, planes_all, points = orbitals.shape
    planes = planes_all // dom
    weights = projector_blocks[0, 0]
    slot_total, row_width, col_width = weights.shape
    halves = points // row_width
    row_blocks = planes * halves
    col_blocks = strengths.shape[0] // col_width
    state_total = local_states * dom

    outgoing = orbitals.reshape(local_states, dom, planes, halves, row_width).transpose(1, 2, 3, 0, 4)
    slab_states = lax.all_to_all(outgoing, "dom", split_axis=0, concat_axis=3, tiled=True)
    slab_states = slab_states.reshape(row_blocks, state_total, row_width)

    slot_rows = block_rows[0, 0]
    slot_cols = block_cols[0, 0]
    live_total = block_counts[0, 0].reshape(1)

    partial_value = project(slot_rows, slot_cols, live_total, slab_states, weights, 3 * col_blocks)
    partial_value = partial_value.reshape(3, col_blocks, state_total, col_width)
    from_below = passed_along(partial_value[2], "dom", 1)
    from_above = passed_along(partial_value[0], "dom", -1)
    own = partial_value[1] + from_below + from_above
    summed = lax.psum(own, "band")
    scaling = strengths.reshape(col_blocks, 1, col_width)
    scaled = (scaling * summed).astype(jnp.bfloat16)
    chi_below = passed_along(scaled, "dom", 1)
    chi_above = passed_along(scaled, "dom", -1)
    neighbours = jnp.concatenate([chi_below, scaled, chi_above], axis=0)

    applied = apply(slot_rows, slot_cols, live_total, neighbours, weights, row_blocks)
    applied = applied.reshape(1, planes, halves, state_total, row_width)
    returned = lax.all_to_all(applied, "dom", split_axis=3, concat_axis=0, tiled=True)
    returned = returned.transpose(3, 0, 1, 2, 4)
    return returned.reshape(local_states, planes_all, points)


def solution(mesh):
    return jax.shard_map(
        per_device,
        mesh=mesh,
        in_specs=(
            P("dom", None, "band"),
            P("band", "dom", None, None, None),
            P("band", "dom", None),
            P("band", "dom", None),
            P("band", "dom"),
            P("dom"),
        ),
        out_specs=P("dom", None, "band"),
        check_vma=False,
    )
```
